32 devices in a mesh: dp: 4 (over z), fsdp: 8 (over y, x, core).
Axes of the slice: x: 2, y: 2, z: 4, core: 2. Of those that a mesh axis runs over, the one named last changes fastest.
Arguments:
- tokens: bfloat16 [4096, 1024], P(('dp', 'fsdp')), may hold values from -6 to 6
- seq_starts: int32 [4, 2], P('dp'), may hold values from 0 to 768, as said below
- expert_ids: int32 [4096, 8], P(('dp', 'fsdp')), may hold values from 0 to 31, all different within a row; in each aligned block of 128 rows (0 to 127, 128 to 255, ...) at most 48 rows name the same one
- attn_gain: bfloat16 [1024], P(('dp', 'fsdp')), may hold values from 0.099609375 to 1.8984375
- w_query: bfloat16 [1024, 1024], P(('dp', 'fsdp')), may hold values from -1 to 1
- key_weight: bfloat16 [1024, 512], P(('dp', 'fsdp')), may hold values from -1 to 1
- value_weight: bfloat16 [1024, 512], P(('dp', 'fsdp')), may hold values from -0.1875 to 0.1875
- w_output: bfloat16 [1024, 1024], P(('dp', 'fsdp')), may hold values from -3 to 3
- ffn_gain: bfloat16 [1024], P(('dp', 'fsdp')), may hold values from 0.099609375 to 1.8984375
- w_router: bfloat16 [1024, 32], P(('dp', 'fsdp')), may hold values from -1 to 1
- expert_in: bfloat16 [32, 1024, 1024], P('fsdp', 'dp'), may hold values from -0.1875 to 0.1875
- expert_out: bfloat16 [32, 512, 1024], P('fsdp', None, 'dp'), may hold values from -0.5 to 0.5
- d_out: bfloat16 [4096, 1024], P(('dp', 'fsdp')), may hold values from -6 to 6
Outputs:
- block_out: bfloat16 [4096, 1024], P(('dp', 'fsdp'))
- d_tokens: float32 [4096, 1024], P(('dp', 'fsdp'))
- d_attn_gain: float32 [1024], P(('dp', 'fsdp'))
- d_query: float32 [1024, 1024], P(('dp', 'fsdp'))
- d_key: float32 [1024, 512], P(('dp', 'fsdp'))
- d_value: float32 [1024, 512], P(('dp', 'fsdp'))
- d_output: float32 [1024, 1024], P(('dp', 'fsdp'))
- d_ffn_gain: float32 [1024], P(('dp', 'fsdp'))
- d_router: float32 [1024, 32], P(('dp', 'fsdp'))
- d_expert_in: float32 [32, 1024, 1024], P('fsdp', 'dp')
- d_expert_out: float32 [32, 512, 1024], P('fsdp', None, 'dp')
The draws below stay inside these ranges and needn't reach their ends.
Inputs may be any that keep to these rules, and one draw needn't show every extreme that they name: seq_starts[g, 0] is 0 and seq_starts[g, 1] splits group g into two sequences of 256 tokens or more (group 0's second sequence has exactly 256). `expert_ids`: each row names 8 different experts; among the 128 rows of one device no expert is named more than 48 times.
All inputs are finite; a program needn't handle non-finite values.
Results may differ from the reference program's by a relative error of at most 0.015.
Values may be sent and summed in bfloat16 or wider, within the bound.
No kernel may reach another device: no remote copies, remote signals or barrier semaphores. Data moves between devices by JAX's collectives and lax.ppermute only.
A program may use at most 192 MiB of HBM per device.

```python
import math
import jax
import jax.numpy as jnp
import numpy as np
from jax import lax

MODEL_DIM = 1024
QUERY_HEADS = 16
KEY_HEADS = 8
HEAD_DIM = 64
EXPERTS = 32
FF = 512
TOP = 8
TOK_DEV = 128
SEQ_MIN = 256
GROUP_TOKENS = 1024
TOKEN_TOTAL = 4096
CAP = 48
N_DP = 4
N_FSDP = 8


def draw_seq_starts(key, part):
    if GROUP_TOKENS >= 2 * SEQ_MIN:
        low_cut = SEQ_MIN
        high_cut = GROUP_TOKENS - SEQ_MIN
    else:
        low_cut = GROUP_TOKENS
        high_cut = GROUP_TOKENS
    cuts = jax.random.randint(key, (N_DP,), low_cut, high_cut + 1).astype(jnp.int32)
    cuts = cuts.at[0].set(high_cut)
    return jnp.stack([jnp.zeros((N_DP,), jnp.int32), cuts], axis=1)


def projection_sample(key, rows_in, cols_out):
    spread = rows_in ** (-0.5)
    return jnp.clip(jax.random.normal(key, (rows_in, cols_out), jnp.float32) * spread, -4.0 * spread, 4.0 * spread)


def draw_w_query(key, part):
    return projection_sample(jax.random.fold_in(key, 11), MODEL_DIM, QUERY_HEADS * HEAD_DIM).astype(jnp.bfloat16)


def draw_key_weight(key, part):
    return projection_sample(jax.random.fold_in(key, 23), MODEL_DIM, KEY_HEADS * HEAD_DIM).astype(jnp.bfloat16)


def draw_w_router(key, part):
    return projection_sample(jax.random.fold_in(key, 37), MODEL_DIM, EXPERTS).astype(jnp.bfloat16)


def raised(array, stream_key, source, target, parts, factor):
    owner, partner = [(jnp.arange(array.shape[position]) // (array.shape[position] // parts)).reshape([-1 if axis == position else 1 for axis in range(array.ndim)]) for position in (source, target)]
    chosen = jax.random.permutation(stream_key, parts)[partner]
    strong = (owner == chosen) | (owner == (partner + parts // 2) % parts)
    return jnp.where(strong, factor * array, array)


def block_levels(key, shape, cuts, least, top_value):
    level, own = 1.0, jax.random.fold_in(key, 6)
    for position, parts in cuts:
        steps = jnp.exp(jax.random.uniform(jax.random.fold_in(own, position), (parts,), jnp.float32, least / len(cuts), top_value / len(cuts)))
        level = level * jnp.repeat(steps, shape[position] // parts).reshape([-1 if axis == position else 1 for axis in range(len(shape))])
    return level


def deal_out(key, own, number, rows, count, top, limit, lean):
    order = jax.random.permutation(key, count)
    crowded, ordinary = shares(count, rows * top, limit, lean, True), shares(count, rows * top, limit, lean, False)
    places = jnp.arange(count)

    def named(lengths, offset_by):
        used = int((lengths > 0).sum())
        fixed = max(1, used // 4)
        passed = fixed + (places - fixed + offset_by * (used - fixed)) % max(1, count - fixed)
        return jnp.zeros((count,), jnp.int32).at[order[jnp.where(places < fixed, places, passed)]].set(jnp.asarray(lengths, jnp.int32))

    lengths = jnp.where(number % 4 == 0, named(crowded, number // 4), named(ordinary, number - number // 4 - 1))
    mixed = jax.random.permutation(jax.random.fold_in(own, 3), count)
    donor, taker = mixed[0:count // 2 * 2:2], mixed[1:count // 2 * 2:2]
    room = jnp.minimum(lengths[donor] - 1, limit - lengths[taker]) // 2
    room = jnp.where((donor == order[0]) | (taker == order[0]) | (lengths[taker] == 0), 0, jnp.maximum(room, 0))
    passed = jax.random.randint(jax.random.fold_in(own, 4), (count // 2,), 0, 1 << 20) % (room + 1)
    lengths = lengths.at[donor].add(-passed).at[taker].add(passed)
    members = jnp.searchsorted(jnp.cumsum(lengths), jnp.arange(rows * top), side="right").astype(jnp.int32)
    grid = members.reshape(top, rows).T
    grid = grid[jax.random.permutation(jax.random.fold_in(own, 1), rows)]
    offset_by = jax.random.randint(jax.random.fold_in(own, 2), (rows, 1), 0, top)
    return jnp.take_along_axis(grid, (jnp.arange(top)[None, :] + offset_by) % top, axis=1)


def shares(count, total, reach, slope, full):
    weights = [(1 << 20) // math.isqrt(rank ** slope) + 1 for rank in range(1, count + 1)]
    largest = reach if full else min(reach, max(-(-total // count), total * weights[0] // sum(weights)))
    least = 1 if total - largest >= count - 1 else 0
    holding, surplus = [largest] + [least] * (count - 1), total - largest - least * (count - 1)
    while surplus > 0:
        movable = [i for i in range(1, count) if holding[i] < largest] or [i for i in range(1, count) if holding[i] < reach]
        mass, budget = sum([weights[i] for i in movable]), surplus
        for i in movable:
            addition = min(reach - holding[i], max(1, budget * weights[i] // mass), surplus)
            holding[i] = holding[i] + addition
            surplus = surplus - addition
    return np.array(holding)


def noise(key, shape, scale, reach, shards=(), kind=jnp.bfloat16):
    values = jax.random.normal(key, shape, jnp.float32) * scale
    if len(shards) > 0:
        values = block_levels(key, shape, shards, -0.22, 0.18) * values
    return jnp.clip(values, min=-reach, max=reach).astype(kind)


def bell_draw_with(key, shape, scale, most, shards, heavy, kind=jnp.bfloat16):
    entries = scale * jax.random.normal(key, shape, jnp.float32)
    if shards:
        entries = entries * block_levels(key, shape, shards, -0.22, 0.18)
    return jnp.clip(raised(entries, jax.random.fold_in(key, 3), *heavy), -most, most).astype(kind)


def setup_inputs(seed: int = 0) -> dict:
    seeds = jax.random.split(jax.random.key(seed), 14)
    tokens = bell_draw_with(seeds[0], (TOKEN_TOTAL, MODEL_DIM), 1.0, 6.0, ((0, 32),), (0, 1, 32, 2.75))
    seq_starts = draw_seq_starts(jax.random.fold_in(seeds[13], 71), 0)
    expert_ids_keys = jax.random.split(jax.random.fold_in(seeds[2], 1), TOKEN_TOTAL // TOK_DEV)
    expert_ids_turns = jax.random.permutation(jax.random.fold_in(seeds[2], 3), TOKEN_TOTAL // TOK_DEV)
    expert_ids = jax.vmap(lambda own, number: deal_out(jax.random.fold_in(seeds[2], 2), own, number, TOK_DEV, EXPERTS, TOP, CAP, 1))(expert_ids_keys, expert_ids_turns).reshape((TOKEN_TOTAL, TOP))
    attn_gain = jnp.clip(1.0 + 0.18 * jax.random.normal(seeds[3], (MODEL_DIM,), jnp.float32), 0.099609375, 1.8984375).astype(jnp.bfloat16)
    w_query = draw_w_query(jax.random.fold_in(seeds[13], 71), 0)
    key_weight = draw_key_weight(jax.random.fold_in(seeds[13], 71), 0)
    value_weight = noise(seeds[6], (MODEL_DIM, KEY_HEADS * HEAD_DIM), MODEL_DIM ** -0.5, 0.1875, ((0, 32),))
    w_output = noise(seeds[7], (QUERY_HEADS * HEAD_DIM, MODEL_DIM), 4 ** -0.5, 3.0, ((0, 32),))
    ffn_gain = jnp.clip(1.0 + 0.18 * jax.random.normal(seeds[8], (MODEL_DIM,), jnp.float32), 0.099609375, 1.8984375).astype(jnp.bfloat16)
    w_router = draw_w_router(jax.random.fold_in(seeds[13], 71), 0)
    expert_in = noise(seeds[10], (EXPERTS, MODEL_DIM, 2 * FF), MODEL_DIM ** -0.5, 0.1875, ((0, 8), (1, 4)))
    expert_out = noise(seeds[11], (EXPERTS, FF, MODEL_DIM), (FF // 4) ** -0.5, 0.5, ((0, 8), (2, 4)))
    d_out = noise(seeds[12], (TOKEN_TOTAL, MODEL_DIM), 1.0, 6.0, ((0, 32),))
    return {"tokens": tokens, "seq_starts": seq_starts, "expert_ids": expert_ids, "attn_gain": attn_gain, "w_query": w_query, "key_weight": key_weight, "value_weight": value_weight, "w_output": w_output, "ffn_gain": ffn_gain, "w_router": w_router, "expert_in": expert_in, "expert_out": expert_out, "d_out": d_out}


norm_eps = 1e-06
score_scale = 0.015625
rope_base = 10000.0

def bround(values):
    return lax.optimization_barrier(values.astype(jnp.bfloat16)).astype(jnp.float32)

def norm_forward(values, gain_vec):
    scale_row = lax.rsqrt(lax.optimization_barrier(jnp.mean(values * values, axis=-1, keepdims=True)) + norm_eps)
    unit_row = values * scale_row
    return (unit_row, scale_row, (unit_row * gain_vec.astype(jnp.float32)).astype(jnp.bfloat16))

def norm_backward(d_normed, unit_row, scale_row, gain_vec):
    scaled = d_normed * gain_vec.astype(jnp.float32)
    grad_values = scale_row * (scaled - unit_row * lax.optimization_barrier(jnp.mean(scaled * unit_row, axis=-1, keepdims=True)))
    return (grad_values, lax.optimization_barrier(jnp.sum(d_normed * unit_row, axis=0)))

def rope_tables(positions):
    half_index = jnp.arange(HEAD_DIM // 2, dtype=jnp.float32)
    inverse = jnp.exp(half_index * (-2.0 * math.log(rope_base) / HEAD_DIM))
    angles = positions.astype(jnp.float32)[:, None] * inverse[None, :]
    return (jnp.cos(angles), jnp.sin(angles))

def apply_rotation(values, cosine_table, sine_values):
    first_half, second_half = jnp.split(values, 2, axis=-1)
    cos_col = cosine_table[:, None, :]
    sin_col = sine_values[:, None, :]
    return jnp.concatenate([first_half * cos_col - second_half * sin_col, second_half * cos_col + first_half * sin_col], axis=-1)

def reverse_rotation(values, cosine_table, sine_values):
    first_half, second_half = jnp.split(values, 2, axis=-1)
    cos_col = cosine_table[:, None, :]
    sin_col = sine_values[:, None, :]
    return jnp.concatenate([first_half * cos_col + second_half * sin_col, second_half * cos_col - first_half * sin_col], axis=-1)

def block_scores(query_block, key_matrix, query_positions, sequence_start):
    current_rows = query_block.shape[0]
    grouped_rows = query_block.astype(jnp.float32).reshape(current_rows, KEY_HEADS, QUERY_HEADS // KEY_HEADS, HEAD_DIM)
    scores = jnp.einsum('tgrd,kgd->tgrk', grouped_rows, key_matrix.astype(jnp.float32)) * score_scale
    key_pos = jnp.arange(GROUP_TOKENS, dtype=jnp.int32)
    allowed = (key_pos[None, :] <= query_positions[:, None]) & (key_pos[None, :] >= sequence_start[:, None])
    return (grouped_rows, scores, allowed[:, None, None, :])

def group_forward(packed):
    query_rows, key_matrix, value_matrix, sequence_start = packed
    rows_per_block = math.gcd(GROUP_TOKENS, 512)
    count_blocks = GROUP_TOKENS // rows_per_block
    query_positions = jnp.arange(GROUP_TOKENS, dtype=jnp.int32)
    value_f32 = value_matrix.astype(jnp.float32)

    def one_block(split_parts):
        query_block, pos_blk, begin_blk = split_parts
        grouped_rows, scores, allowed = block_scores(query_block, key_matrix, pos_blk, begin_blk)
        row_max = lax.optimization_barrier(jnp.max(jnp.where(allowed, scores, -jnp.inf), axis=-1, keepdims=True))
        summed = lax.optimization_barrier(jnp.sum(jnp.where(allowed, jnp.exp(scores - row_max), 0.0), axis=-1, keepdims=True))
        log_sum_exponent = row_max + jnp.log(summed)
        probs = bround(jnp.where(allowed, jnp.exp(scores - log_sum_exponent), 0.0))
        attended_rows = jnp.einsum('tgrk,kgd->tgrd', probs, value_f32)
        return (attended_rows.reshape(rows_per_block, QUERY_HEADS * HEAD_DIM).astype(jnp.bfloat16), log_sum_exponent[..., 0])
    attended_rows, log_sum_exponent = lax.map(one_block, (query_rows.reshape(count_blocks, rows_per_block, QUERY_HEADS, HEAD_DIM), query_positions.reshape(count_blocks, rows_per_block), sequence_start.reshape(count_blocks, rows_per_block)))
    return (attended_rows.reshape(GROUP_TOKENS, QUERY_HEADS * HEAD_DIM), log_sum_exponent.reshape(GROUP_TOKENS, KEY_HEADS, QUERY_HEADS // KEY_HEADS))

def group_backward(packed):
    query_rows, key_matrix, value_matrix, sequence_start, log_sum_exponent, grad_attended, attended_rows = packed
    rows_per_block = math.gcd(GROUP_TOKENS, 512)
    count_blocks = GROUP_TOKENS // rows_per_block
    heads_per_key = QUERY_HEADS // KEY_HEADS
    query_positions = jnp.arange(GROUP_TOKENS, dtype=jnp.int32)
    key_f32 = key_matrix.astype(jnp.float32)
    value_f32 = value_matrix.astype(jnp.float32)

    def one_block(state_pair, split_parts):
        grad_keys, grad_values = state_pair
        query_block, pos_blk, begin_blk, lse_blk, grad_output_block, output_block = split_parts
        grouped_rows, scores, allowed = block_scores(query_block, key_matrix, pos_blk, begin_blk)
        probs = jnp.where(allowed, jnp.exp(scores - lse_blk[..., None]), 0.0)
        grad_grouped = grad_output_block.astype(jnp.float32).reshape(rows_per_block, KEY_HEADS, heads_per_key, HEAD_DIM)
        output_dot_grad = lax.optimization_barrier(jnp.sum(grad_grouped * output_block.astype(jnp.float32).reshape(rows_per_block, KEY_HEADS, heads_per_key, HEAD_DIM), axis=-1))
        grad_values = grad_values + jnp.einsum('tgrk,tgrd->kgd', bround(probs), grad_grouped)
        d_probs = jnp.einsum('tgrd,kgd->tgrk', grad_grouped, value_f32)
        d_scores = bround(probs * (d_probs - output_dot_grad[..., None]) * score_scale)
        d_query_blk = jnp.einsum('tgrk,kgd->tgrd', d_scores, key_f32)
        grad_keys = grad_keys + jnp.einsum('tgrk,tgrd->kgd', d_scores, grouped_rows)
        return ((grad_keys, grad_values), d_query_blk.reshape(rows_per_block, QUERY_HEADS, HEAD_DIM))
    zero_key_values = jnp.zeros((GROUP_TOKENS, KEY_HEADS, HEAD_DIM), jnp.float32)
    split_parts = (query_rows.reshape(count_blocks, rows_per_block, QUERY_HEADS, HEAD_DIM), query_positions.reshape(count_blocks, rows_per_block), sequence_start.reshape(count_blocks, rows_per_block), log_sum_exponent.reshape(count_blocks, rows_per_block, KEY_HEADS, heads_per_key), grad_attended.reshape(count_blocks, rows_per_block, QUERY_HEADS * HEAD_DIM), attended_rows.reshape(count_blocks, rows_per_block, QUERY_HEADS * HEAD_DIM))
    (grad_keys, grad_values), d_queries = lax.scan(one_block, (zero_key_values, zero_key_values), split_parts)
    return (d_queries.reshape(GROUP_TOKENS, QUERY_HEADS, HEAD_DIM), grad_keys, grad_values)

def reference(tokens, seq_starts, expert_ids, attn_gain, w_query, key_weight, value_weight, w_output, ffn_gain, w_router, expert_in, expert_out, d_out):
    tok_f32 = tokens.astype(jnp.float32)
    unit_one, scale_one, first_normed = norm_forward(tok_f32, attn_gain)
    token_idx = jnp.arange(TOKEN_TOTAL, dtype=jnp.int32)
    group_idx = token_idx // GROUP_TOKENS
    in_group = token_idx % GROUP_TOKENS
    second_start = seq_starts[group_idx, 1]
    sequence_start = jnp.where(in_group >= second_start, second_start, seq_starts[group_idx, 0]).astype(jnp.int32)
    cosine_table, sine_values = rope_tables(in_group - sequence_start)
    query_rows = apply_rotation(jnp.dot(first_normed, w_query, preferred_element_type=jnp.float32).reshape(TOKEN_TOTAL, QUERY_HEADS, HEAD_DIM), cosine_table, sine_values).astype(jnp.bfloat16)
    key_matrix = apply_rotation(jnp.dot(first_normed, key_weight, preferred_element_type=jnp.float32).reshape(TOKEN_TOTAL, KEY_HEADS, HEAD_DIM), cosine_table, sine_values).astype(jnp.bfloat16)
    value_matrix = jnp.dot(first_normed, value_weight, preferred_element_type=jnp.float32).astype(jnp.bfloat16).reshape(TOKEN_TOTAL, KEY_HEADS, HEAD_DIM)
    group_q = query_rows.reshape(N_DP, GROUP_TOKENS, QUERY_HEADS, HEAD_DIM)
    group_keys = key_matrix.reshape(N_DP, GROUP_TOKENS, KEY_HEADS, HEAD_DIM)
    group_values = value_matrix.reshape(N_DP, GROUP_TOKENS, KEY_HEADS, HEAD_DIM)
    group_begin = sequence_start.reshape(N_DP, GROUP_TOKENS)
    attended_rows, log_sum_exponent = lax.map(group_forward, (group_q, group_keys, group_values, group_begin))
    attended_rows = attended_rows.reshape(TOKEN_TOTAL, QUERY_HEADS * HEAD_DIM)
    hidden = tok_f32 + jnp.dot(attended_rows, w_output, preferred_element_type=jnp.float32)
    unit_two, scale_two, normed_two = norm_forward(hidden, ffn_gain)
    logits = jnp.dot(normed_two, w_router, preferred_element_type=jnp.float32)
    gate_vals = jax.nn.softmax(jnp.take_along_axis(logits, expert_ids, axis=1), axis=-1)
    devices_all = N_DP * N_FSDP
    one_hot = (expert_ids[:, :, None] == jnp.arange(EXPERTS, dtype=jnp.int32)[None, None, :]).astype(jnp.int32)
    flat_hot = one_hot.reshape(devices_all, TOK_DEV * TOP, EXPERTS)
    before = (jnp.cumsum(flat_hot, axis=1) - flat_hot).astype(jnp.int32)
    slot_pos = lax.optimization_barrier(jnp.sum(before * flat_hot, axis=2)).astype(jnp.int32).reshape(TOKEN_TOTAL, TOP)
    dev_index = token_idx // TOK_DEV
    slots_all = devices_all * CAP
    flat_pos = ((expert_ids * devices_all + dev_index[:, None]) * CAP + slot_pos).astype(jnp.int32).reshape(-1)
    token_table = jnp.full((EXPERTS * slots_all,), TOKEN_TOTAL, dtype=jnp.int32).at[flat_pos].set(jnp.repeat(token_idx, TOP)).reshape(EXPERTS, slots_all)
    gate_table = jnp.zeros((EXPERTS * slots_all,), jnp.float32).at[flat_pos].set(gate_vals.reshape(-1)).reshape(EXPERTS, slots_all)
    normed_pad = jnp.concatenate([normed_two, jnp.zeros((1, MODEL_DIM), jnp.bfloat16)], axis=0)

    def expert_forward(mixture, packed):
        rows_idx, gate_col, weight_in, weight_out = packed
        current_rows = normed_pad[rows_idx]
        gate_up = jnp.dot(current_rows, weight_in, preferred_element_type=jnp.float32)
        gate_part, up_part = jnp.split(gate_up, 2, axis=-1)
        activation = (jax.nn.silu(gate_part) * up_part).astype(jnp.bfloat16)
        result = jnp.dot(activation, weight_out, preferred_element_type=jnp.float32).astype(jnp.bfloat16)
        mixture = mixture.at[rows_idx].add(gate_col[:, None] * result.astype(jnp.float32))
        return (mixture, None)
    mixture, unused = lax.scan(expert_forward, jnp.zeros((TOKEN_TOTAL + 1, MODEL_DIM), jnp.float32), (token_table, gate_table, expert_in, expert_out))
    block_out = (hidden + mixture[:TOKEN_TOTAL]).astype(jnp.bfloat16)
    d_block = d_out.astype(jnp.float32)
    d_pad = jnp.concatenate([d_block, jnp.zeros((1, MODEL_DIM), jnp.float32)], axis=0)

    def expert_backward(d_rows_acc, packed):
        rows_idx, gate_col, weight_in, weight_out = packed
        current_rows = normed_pad[rows_idx]
        gate_up = jnp.dot(current_rows, weight_in, preferred_element_type=jnp.float32)
        gate_part, up_part = jnp.split(gate_up, 2, axis=-1)
        activation = (jax.nn.silu(gate_part) * up_part).astype(jnp.bfloat16)
        result = jnp.dot(activation, weight_out, preferred_element_type=jnp.float32).astype(jnp.bfloat16)
        d_here = d_pad[rows_idx]
        d_result = (gate_col[:, None] * d_here).astype(jnp.bfloat16)
        d_gate_slot = lax.optimization_barrier(jnp.sum(d_here * result.astype(jnp.float32), axis=-1))
        d_act = jnp.dot(d_result, weight_out.T, preferred_element_type=jnp.float32)
        sigmoid_g = jax.nn.sigmoid(gate_part)
        silu_g = gate_part * sigmoid_g
        d_gate_up = jnp.concatenate([d_act * up_part * sigmoid_g * (1.0 + gate_part * (1.0 - sigmoid_g)), d_act * silu_g], axis=-1).astype(jnp.bfloat16)
        grad_out = jnp.dot(activation.T, d_result, preferred_element_type=jnp.float32)
        grad_in = jnp.dot(current_rows.T, d_gate_up, preferred_element_type=jnp.float32)
        d_rows = jnp.dot(d_gate_up, weight_in.T, preferred_element_type=jnp.float32).astype(jnp.bfloat16)
        d_rows_acc = d_rows_acc.at[rows_idx].add(d_rows.astype(jnp.float32))
        return (d_rows_acc, (grad_in, grad_out, d_gate_slot))
    d_rows_acc, (d_expert_in, d_expert_out, d_gate_slots) = lax.scan(expert_backward, jnp.zeros((TOKEN_TOTAL + 1, MODEL_DIM), jnp.float32), (token_table, gate_table, expert_in, expert_out))
    d_gate = d_gate_slots.reshape(-1)[flat_pos].reshape(TOKEN_TOTAL, TOP)
    d_sel = gate_vals * (d_gate - lax.optimization_barrier(jnp.sum(gate_vals * d_gate, axis=-1, keepdims=True)))
    d_logits = lax.optimization_barrier(jnp.sum(one_hot.astype(jnp.float32) * d_sel[:, :, None], axis=1)).astype(jnp.bfloat16)
    d_router = jnp.dot(normed_two.T, d_logits, preferred_element_type=jnp.float32)
    d_normed_two = d_rows_acc[:TOKEN_TOTAL] + jnp.dot(d_logits, w_router.T, preferred_element_type=jnp.float32)
    d_hidden_two, d_ffn_gain = norm_backward(d_normed_two, unit_two, scale_two, ffn_gain)
    d_hidden = d_block + d_hidden_two
    d_hidden_b = d_hidden.astype(jnp.bfloat16)
    d_output = jnp.dot(attended_rows.T, d_hidden_b, preferred_element_type=jnp.float32)
    grad_attended = jnp.dot(d_hidden_b, w_output.T, preferred_element_type=jnp.float32).astype(jnp.bfloat16)
    d_queries, grad_keys, grad_values = lax.map(group_backward, (group_q, group_keys, group_values, group_begin, log_sum_exponent, grad_attended.reshape(N_DP, GROUP_TOKENS, QUERY_HEADS * HEAD_DIM), attended_rows.reshape(N_DP, GROUP_TOKENS, QUERY_HEADS * HEAD_DIM)))
    d_query_b = reverse_rotation(d_queries.reshape(TOKEN_TOTAL, QUERY_HEADS, HEAD_DIM), cosine_table, sine_values).reshape(TOKEN_TOTAL, QUERY_HEADS * HEAD_DIM).astype(jnp.bfloat16)
    grad_key_block = reverse_rotation(grad_keys.reshape(TOKEN_TOTAL, KEY_HEADS, HEAD_DIM), cosine_table, sine_values).reshape(TOKEN_TOTAL, KEY_HEADS * HEAD_DIM).astype(jnp.bfloat16)
    grad_value_block = grad_values.reshape(TOKEN_TOTAL, KEY_HEADS * HEAD_DIM).astype(jnp.bfloat16)
    d_query = jnp.dot(first_normed.T, d_query_b, preferred_element_type=jnp.float32)
    d_key = jnp.dot(first_normed.T, grad_key_block, preferred_element_type=jnp.float32)
    d_value = jnp.dot(first_normed.T, grad_value_block, preferred_element_type=jnp.float32)
    d_normed_one = jnp.dot(d_query_b, w_query.T, preferred_element_type=jnp.float32) + jnp.dot(grad_key_block, key_weight.T, preferred_element_type=jnp.float32) + jnp.dot(grad_value_block, value_weight.T, preferred_element_type=jnp.float32)
    d_tok_one, d_attn_gain = norm_backward(d_normed_one, unit_one, scale_one, attn_gain)
    d_tokens = d_hidden + d_tok_one
    return (block_out, d_tokens, d_attn_gain, d_query, d_key, d_value, d_output, d_ffn_gain, d_router, d_expert_in, d_expert_out)
```

```python
import math

import jax
import jax.numpy as jnp
from jax import lax
from jax.experimental import pallas as pl
from jax.experimental.pallas import tpu as pltpu
from jax.sharding import PartitionSpec as P


QUERY_HEADS = 16
KEY_HEADS = 8
HEAD_DIM = 64
CAP = 48
POOL_PLANES = 2
POOL_SHARDS = 16
PAD = 128


norm_eps = 1e-06
score_scale = 0.015625
rope_base = 10000.0
masked_low = -1e30

f32 = jnp.float32
bf16 = jnp.bfloat16


def swap(values, axis, mask):
    count = lax.axis_size(axis)
    return lax.ppermute(values, axis, [(i, i ^ mask) for i in range(count)])


def dot(left, right, dims):
    return lax.dot_general(left, right, (dims, ((), ())), preferred_element_type=f32)


def norm_backward(d_normed, unit_row, scale_row, gain_row):
    scaled = d_normed * gain_row
    grad_values = scale_row * (
        scaled - unit_row * jnp.mean(scaled * unit_row, axis=-1, keepdims=True)
    )
    return (grad_values, jnp.sum(d_normed * unit_row, axis=0))


def rope_tables(positions, head_size):
    half_index = jnp.arange(head_size // 2, dtype=f32)
    inverse = jnp.exp(half_index * (-2.0 * math.log(rope_base) / head_size))
    angles = positions.astype(f32)[:, None] * inverse[None, :]
    return (jnp.cos(angles), jnp.sin(angles))


def apply_rotation(values, cosine_table, sine_values):
    first_half, second_half = jnp.split(values, 2, axis=-1)
    cos_col = cosine_table[:, None, :]
    sin_col = sine_values[:, None, :]
    return jnp.concatenate(
        [
            first_half * cos_col - second_half * sin_col,
            second_half * cos_col + first_half * sin_col,
        ],
        axis=-1,
    )


def ordered(pieces, index):
    if len(pieces) == 1:
        return pieces
    half = len(pieces) // 2
    low, high = ordered(pieces[:half], index), ordered(pieces[half:], index)
    flip = (index & half) != 0
    return [jnp.where(flip, y, x) for x, y in zip(low, high)] + [
        jnp.where(flip, x, y) for x, y in zip(low, high)
    ]


def chip_masks():
    return [2 * c for c in range(1, lax.axis_size("fsdp") // 2)]


def gather_planes(rows, count):
    if count == 1:
        return rows
    pieces = [rows] + [swap(rows, "dp", k) for k in range(1, count)]
    return jnp.concatenate(pieces, axis=0)


def gather_pieces(rows, planes):
    first = gather_planes(rows, planes)
    half = [first] + [swap(first, "fsdp", m) for m in chip_masks()]
    return half + [swap(piece, "fsdp", 1) for piece in half]


def after(values, event):
    return values if event is None else lax.optimization_barrier((values, event))[0]


def scatter_chips(own_half, other_half, lead, event=None):
    total = own_half.astype(f32) + swap(other_half.astype(bf16), "fsdp", 1).astype(f32)
    parts = total.astype(bf16)
    out = total[:lead]
    for c, m in enumerate(chip_masks(), 1):
        piece = swap(parts[c * lead : (c + 1) * lead], "fsdp", m)
        piece = after(piece, event)
        out = out + piece.astype(f32)
    return out


def scatter_all(own_half, other_half, rows, count, events=(None, None)):
    planes = scatter_chips(own_half, other_half, count * rows, events[0])
    parts = planes.astype(bf16)
    out = planes[:rows]
    for k in range(1, count):
        piece = swap(parts[k * rows : (k + 1) * rows], "dp", k)
        out = out + after(piece, events[1]).astype(f32)
    return out


def gather_rows(rows, planes):
    first = gather_planes(rows, planes)
    half = jnp.concatenate([first] + [swap(first, "fsdp", m) for m in chip_masks()], axis=0)
    return [half, swap(half, "fsdp", 1)]


def expert_kernel(pieces, planes, held, tok_rows, width, ff, experts_total):
    blocks = pieces * planes
    half = pieces // 2
    contract_last = ((1,), (1,))
    contract_first = ((0,), (0,))

    def mm(left, right, dims=((1,), (0,))):
        return lax.dot_general(left, right, (dims, ((), ())), preferred_element_type=f32)

    def kernel(*refs):
        first_ref, router_ref, chosen_ref, slot_ref, win_ref, wout_ref = refs[:6]
        tok_refs = refs[6 : 6 + pieces]
        cot_refs = refs[6 + pieces : 6 + 2 * pieces]
        outs = refs[6 + 2 * pieces :]
        back_refs, mix_refs = outs[0:2], outs[2:4]
        gin_ref, gout_ref, rows_ref, drows_ref, gate_ref, back_rows_ref, mix_rows_ref = outs[4:]
        first = first_ref[0]
        slot_axis = lax.broadcasted_iota(jnp.int32, (CAP, tok_rows), 0)
        expert_axis = lax.broadcasted_iota(jnp.int32, (experts_total, planes * tok_rows), 0)

        def selection(block):
            return [slot_axis == slot_ref[block, e : e + 1, :] for e in range(held)]

        def stacked(parts):
            parts = [x.astype(f32) for x in parts]
            out = parts[0] if held == 1 else jnp.concatenate(parts, axis=0)
            return out.astype(bf16)

        for i in range(pieces):
            logits = mm(router_ref[...], tok_refs[i][...], contract_last)
            chosen = chosen_ref[i] > 0.0
            top = jnp.max(jnp.where(chosen, logits, masked_low), axis=0, keepdims=True)
            raised = jnp.where(chosen, jnp.exp(logits - top), 0.0)
            gates = raised / jnp.sum(raised, axis=0, keepdims=True)
            mine = [
                jnp.sum(jnp.where(expert_axis == first + e, gates, 0.0), axis=0, keepdims=True)
                for e in range(held)
            ]
            for a in range(planes):
                block = i * planes + a
                at = slice(a * tok_rows, (a + 1) * tok_rows)
                picks = selection(block)
                for e in range(held):
                    gate_ref[e, block * CAP : (block + 1) * CAP, :] = jnp.sum(
                        jnp.where(picks[e], mine[e][:, at], 0.0), axis=1, keepdims=True
                    )
                pick = stacked(picks)
                rows_ref[block] = mm(pick, tok_refs[i][at, :]).astype(bf16)
                drows_ref[block] = mm(pick, cot_refs[i][at, :width]).astype(bf16)

        lane = lax.broadcasted_iota(jnp.int32, (blocks * CAP, PAD), 1)
        for e in range(held):
            strip = slice(e * CAP, (e + 1) * CAP)
            rows = rows_ref[:, strip, :].reshape(blocks * CAP, width)
            gate = gate_ref[e]
            gate_up = mm(rows, win_ref[e])
            gate_part, up_part = gate_up[:, :ff], gate_up[:, ff:]
            sigmoid_g = 1.0 / (1.0 + jnp.exp(-gate_part))
            silu_g = gate_part * sigmoid_g
            activation = (silu_g * up_part).astype(bf16)
            result = mm(activation, wout_ref[e]).astype(bf16).astype(f32)
            mix_rows_ref[:, strip, :] = (gate * result).astype(bf16).reshape(blocks, CAP, width)
            d_rows = drows_ref[:, strip, :].reshape(blocks * CAP, width).astype(f32)
            d_gate = jnp.sum(d_rows * result, axis=1, keepdims=True)
            high = d_gate.astype(bf16).astype(f32)
            cols = jnp.where(
                lane == first + e,
                high,
                jnp.where(lane == first + e + experts_total, d_gate - high, 0.0),
            )
            back_rows_ref[:, strip, width:] = cols.astype(bf16).reshape(blocks, CAP, PAD)
            d_result = (gate * d_rows).astype(bf16)
            gout_ref[e] = mm(activation, d_result, contract_first).astype(bf16)
            d_act = mm(d_result, wout_ref[e], contract_last)
            d_gate_up = jnp.concatenate(
                [
                    d_act * up_part * sigmoid_g * (1.0 + gate_part * (1.0 - sigmoid_g)),
                    d_act * silu_g,
                ],
                axis=1,
            ).astype(bf16)
            back_rows_ref[:, strip, :width] = (
                mm(d_gate_up, win_ref[e], contract_last).astype(bf16).reshape(blocks, CAP, width)
            )
            gin_ref[e] = mm(rows, d_gate_up, contract_first).astype(bf16)

        for block in range(blocks):
            pick = stacked(selection(block))
            side, place = divmod(block, half * planes)
            at = slice(place * tok_rows, (place + 1) * tok_rows)
            back_refs[side][at, :] = mm(pick, back_rows_ref[block], contract_first).astype(bf16)
            mix_refs[side][at, :] = mm(pick, mix_rows_ref[block], contract_first).astype(bf16)

    side_rows = half * planes * tok_rows
    in_vmem = pl.BlockSpec(memory_space=pltpu.VMEM)
    return pl.pallas_call(
        kernel,
        out_shape=[jax.ShapeDtypeStruct((side_rows, width + PAD), bf16)] * 2
        + [jax.ShapeDtypeStruct((side_rows, width), bf16)] * 2
        + [
            jax.ShapeDtypeStruct((held, width, 2 * ff), bf16),
            jax.ShapeDtypeStruct((held, ff, width), bf16),
        ],
        in_specs=[pl.BlockSpec(memory_space=pltpu.SMEM)] + [in_vmem] * (5 + 2 * pieces),
        out_specs=[in_vmem] * 6,
        scratch_shapes=[
            pltpu.VMEM((blocks, held * CAP, width), bf16),
            pltpu.VMEM((blocks, held * CAP, width), bf16),
            pltpu.VMEM((held, blocks * CAP, 1), f32),
            pltpu.VMEM((blocks, held * CAP, width + PAD), bf16),
            pltpu.VMEM((blocks, held * CAP, width), bf16),
        ],
        compiler_params=pltpu.CompilerParams(vmem_limit_bytes=60 * 1024 * 1024),
        name="experts",
    )


def local(
    tokens,
    seq_starts,
    expert_ids,
    attn_gain,
    w_query,
    key_weight,
    value_weight,
    w_output,
    ffn_gain,
    w_router,
    expert_in,
    expert_out,
    d_out,
):
    fsdp_count = lax.axis_size("fsdp")
    dp_count = lax.axis_size("dp")
    fsdp_at = lax.axis_index("fsdp")
    dp_at = lax.axis_index("dp")
    chips = fsdp_count // 2
    tok_rows, width = tokens.shape
    own_rows = w_query.shape[0]
    local_experts, slice_width, ff_two = expert_in.shape
    ff = ff_two // 2
    experts_total = w_router.shape[1]
    planes = POOL_PLANES
    if local_experts % planes or dp_count % planes or planes * fsdp_count > POOL_SHARDS:
        planes = 1
    held = local_experts // planes
    heads_per_key = QUERY_HEADS // KEY_HEADS
    q_width = QUERY_HEADS * HEAD_DIM
    kv_width = KEY_HEADS * HEAD_DIM

    pack_one = jnp.concatenate(
        [w_query, key_weight, value_weight, attn_gain[:, None], jnp.zeros((own_rows, PAD - 1), bf16)],
        axis=1,
    )
    pack_two = jnp.concatenate(
        [
            w_output,
            w_router,
            ffn_gain[:, None],
            jnp.zeros((own_rows, PAD - experts_total - 1), bf16),
        ],
        axis=1,
    )
    qkv_pieces = gather_pieces(pack_one, dp_count)
    output_own, output_other = gather_rows(pack_two, dp_count)

    rel = jnp.arange(width, dtype=jnp.int32)
    rel_row = rel % own_rows
    rel_dp = (rel // own_rows) % dp_count
    rel_chip = (rel // (own_rows * dp_count)) % chips
    rel_core = rel // (own_rows * dp_count * chips)
    place = (
        (rel_dp ^ dp_at) * fsdp_count + ((2 * rel_chip + rel_core) ^ fsdp_at)
    ) * own_rows + rel_row
    shuffle = (place[None, :] == jnp.arange(width, dtype=jnp.int32)[:, None]).astype(bf16)
    half_width = width // 2

    small_own, small_other = output_own[:, width:], output_other[:, width:]
    small_all = (
        dot(shuffle[:, :half_width], small_own, ((1,), (0,)))
        + dot(shuffle[:, half_width:], small_other, ((1,), (0,)))
    ).astype(bf16)
    router_w = small_all[:, :experts_total]
    gain_two = small_all[:, experts_total].astype(f32)[None, :]

    d_pack = jnp.concatenate(
        [d_out, expert_ids.astype(bf16), jnp.zeros((tok_rows, PAD - expert_ids.shape[1]), bf16)],
        axis=1,
    )
    d_pool = gather_pieces(d_pack, planes)

    group_at = dp_at % planes
    in_groups = expert_in.reshape(planes, held, slice_width, ff_two)
    out_groups = expert_out.reshape(planes, held, ff, slice_width)
    in_parts, out_parts = [], []
    for k in range(dp_count):
        target = group_at ^ (k % planes)
        in_piece = lax.dynamic_index_in_dim(in_groups, target, 0, keepdims=False)
        out_piece = lax.dynamic_index_in_dim(out_groups, target, 0, keepdims=False)
        in_parts.append(in_piece if k == 0 else swap(in_piece, "dp", k))
        out_parts.append(out_piece if k == 0 else swap(out_piece, "dp", k))
    token_index = jnp.arange(tok_rows, dtype=jnp.int32)
    global_pos = fsdp_at * tok_rows + token_index
    second_start = seq_starts[0, 1]
    sequence_start = jnp.where(global_pos >= second_start, second_start, seq_starts[0, 0])
    cosine_table, sine_values = rope_tables(global_pos - sequence_start, HEAD_DIM)
    tok_f32 = tokens.astype(f32)
    scale_one = lax.rsqrt(jnp.mean(tok_f32 * tok_f32, axis=-1, keepdims=True) + norm_eps)
    unit_one = dot(tokens, shuffle, ((1,), (0,))) * scale_one
    gain_col = q_width + 2 * kv_width
    gain_one = jnp.concatenate([piece[:, gain_col] for piece in qkv_pieces]).astype(f32)[None, :]
    first_normed = (unit_one * gain_one).astype(bf16)
    projected = sum(
        dot(first_normed[:, i * piece.shape[0] : (i + 1) * piece.shape[0]], piece, ((1,), (0,)))
        for i, piece in enumerate(qkv_pieces)
    )
    query_rows = apply_rotation(
        projected[:, :q_width].reshape(tok_rows, QUERY_HEADS, HEAD_DIM), cosine_table, sine_values
    ).astype(bf16)
    key_rows = apply_rotation(
        projected[:, q_width : q_width + kv_width].reshape(tok_rows, KEY_HEADS, HEAD_DIM),
        cosine_table,
        sine_values,
    ).astype(bf16)
    value_rows = projected[:, q_width + kv_width : q_width + 2 * kv_width].astype(bf16)
    kv_rows = jnp.concatenate([key_rows.reshape(tok_rows, kv_width), value_rows], axis=1)
    kv_all = jnp.concatenate(gather_rows(kv_rows, 1), axis=0)
    shard = jnp.arange(fsdp_count, dtype=jnp.int32)
    shard_dev = (2 * (shard % chips) + shard // chips) ^ fsdp_at
    key_pos = (shard_dev[:, None] * tok_rows + token_index[None, :]).reshape(-1)
    allowed = (key_pos[None, :] <= global_pos[:, None]) & (
        key_pos[None, :] >= sequence_start[:, None]
    )
    keys = kv_all[:, :kv_width].reshape(-1, KEY_HEADS, HEAD_DIM)
    vals = kv_all[:, kv_width:].reshape(-1, KEY_HEADS, HEAD_DIM)
    grouped = query_rows.reshape(tok_rows, KEY_HEADS, heads_per_key, HEAD_DIM)
    mask = allowed[None, None]
    scores = (
        jnp.einsum("tgrd,kgd->grtk", grouped, keys, preferred_element_type=f32) * score_scale
    )
    row_max = jnp.max(jnp.where(mask, scores, masked_low), axis=-1, keepdims=True)
    summed = jnp.sum(jnp.where(mask, jnp.exp(scores - row_max), 0.0), axis=-1, keepdims=True)
    lse = row_max + jnp.log(summed)
    probs = jnp.where(mask, jnp.exp(scores - lse), 0.0)
    probs_b = probs.astype(bf16)
    attended = jnp.einsum("grtk,kgd->tgrd", probs_b, vals, preferred_element_type=f32).astype(bf16)
    attended_rows = attended.reshape(tok_rows, q_width)
    attended_rel = dot(attended_rows, shuffle, ((1,), (0,))).astype(bf16)
    hidden = tok_f32 + (
        dot(attended_rel[:, :half_width], output_own[:, :width], ((1,), (0,)))
        + dot(attended_rel[:, half_width:], output_other[:, :width], ((1,), (0,)))
    )
    scale_two = lax.rsqrt(jnp.mean(hidden * hidden, axis=-1, keepdims=True) + norm_eps)
    unit_two = hidden * scale_two
    normed_two = (unit_two * gain_two).astype(bf16)

    normed_pool = gather_pieces(normed_two, planes)
    win = jnp.zeros((held, width, ff_two), bf16)
    for k in range(dp_count):
        win = lax.dynamic_update_slice(win, in_parts[k], (0, (dp_at ^ k) * slice_width, 0))
    wout = jnp.concatenate(ordered(out_parts, dp_at), axis=2)
    expert_axis = jnp.arange(experts_total, dtype=jnp.int32)
    first_expert = fsdp_at * local_experts + group_at * held
    my_experts = first_expert + jnp.arange(held, dtype=jnp.int32)
    lower = (token_index[:, None] > token_index[None, :]).astype(bf16)

    def dense_gates(rows, chosen):
        logits = dot(rows, router_w, ((1,), (0,)))
        top = jnp.max(jnp.where(chosen, logits, masked_low), axis=-1, keepdims=True)
        raised = jnp.where(chosen, jnp.exp(logits - top), 0.0)
        return raised / jnp.sum(raised, axis=-1, keepdims=True)

    def chosen_of(ids):
        return jnp.any(ids[:, :, None] == expert_axis[None, None, :], axis=1)

    pieces = len(normed_pool)
    ids_all = jnp.stack([x[:, width : width + expert_ids.shape[1]] for x in d_pool])
    ids_all = ids_all.astype(jnp.int32)
    chosen_rows = (
        jnp.any(ids_all[:, None] == expert_axis[None, :, None, None], axis=-1).astype(f32)
    )
    mine = jnp.any(ids_all[:, None] == my_experts[None, :, None, None], axis=-1)
    mine = mine.reshape(pieces, held, planes, tok_rows)
    before = jnp.einsum(
        "iepu,tu->iept", mine.astype(bf16), lower, preferred_element_type=f32
    ).astype(jnp.int32)
    slots = jnp.where(mine, before, -1).transpose(0, 2, 1, 3).reshape(-1, held, tok_rows)
    run = expert_kernel(pieces, planes, held, tok_rows, width, ff, experts_total)
    back_own, back_other, mix_own, mix_other, grad_in_b, grad_out_b = run(
        first_expert[None], router_w.T, chosen_rows, slots, win, wout, *normed_pool, *d_pool
    )
    back = scatter_all(back_own, back_other, tok_rows, planes)

    in_sent, out_sent = [], []
    for k in range(dp_count):
        target = dp_at ^ k
        in_piece = lax.dynamic_slice_in_dim(grad_in_b, target * slice_width, slice_width, 1)
        out_piece = lax.dynamic_slice_in_dim(grad_out_b, target * slice_width, slice_width, 2)
        if k:
            in_piece, out_piece = swap(in_piece, "dp", k), swap(out_piece, "dp", k)
        in_sent.append(in_piece)
        out_sent.append(out_piece)

    d_block = d_out.astype(f32)
    d_gate = (
        back[:, width : width + experts_total]
        + back[:, width + experts_total : width + 2 * experts_total]
    )
    gates = dense_gates(normed_two, chosen_of(expert_ids))
    d_logits = (gates * (d_gate - jnp.sum(gates * d_gate, axis=-1, keepdims=True))).astype(bf16)
    d_normed_two = back[:, :width] + dot(d_logits, router_w, ((1,), (1,)))
    d_hidden_two, grad_gain_two = norm_backward(d_normed_two, unit_two, scale_two, gain_two)
    d_hidden = d_block + d_hidden_two
    d_hidden_b = d_hidden.astype(bf16)
    normed_two_rel = dot(normed_two, shuffle, ((1,), (0,))).astype(bf16)
    gain_two_rel = jnp.dot(
        grad_gain_two[None, :], shuffle.astype(f32), precision=lax.Precision.HIGHEST
    )[0]
    grad_output_own = dot(attended_rel[:, :half_width], d_hidden_b, ((0,), (0,)))
    grad_output_other = dot(attended_rel[:, half_width:], d_hidden_b, ((0,), (0,))).astype(bf16)
    grad_router_rel = dot(normed_two_rel, d_logits, ((0,), (0,)))

    grad_attended_rel = jnp.concatenate(
        [
            dot(d_hidden_b, output_own[:, :width], ((1,), (1,))),
            dot(d_hidden_b, output_other[:, :width], ((1,), (1,))),
        ],
        axis=1,
    ).astype(bf16)
    grad_attended = dot(grad_attended_rel, shuffle, ((1,), (1,))).astype(bf16)
    grad_grouped = grad_attended.reshape(tok_rows, KEY_HEADS, heads_per_key, HEAD_DIM)
    delta = jnp.sum(grad_grouped.astype(f32) * attended.astype(f32), axis=-1).transpose(1, 2, 0)
    d_vals = jnp.einsum("grtk,tgrd->kgd", probs_b, grad_grouped, preferred_element_type=f32)
    d_probs = jnp.einsum("tgrd,kgd->grtk", grad_grouped, vals, preferred_element_type=f32)
    d_scores = (probs * (d_probs - delta[..., None]) * score_scale).astype(bf16)
    d_queries = jnp.einsum("grtk,kgd->tgrd", d_scores, keys, preferred_element_type=f32)
    d_keys = jnp.einsum("grtk,tgrd->kgd", d_scores, grouped, preferred_element_type=f32)
    d_kv = jnp.concatenate([d_keys.reshape(-1, kv_width), d_vals.reshape(-1, kv_width)], axis=1)
    split_at = chips * tok_rows
    d_kv_own = scatter_chips(d_kv[:split_at], d_kv[split_at:].astype(bf16), tok_rows)
    summed_output = scatter_all(grad_output_own, grad_output_other, own_rows, dp_count)
    d_query_b = apply_rotation(
        d_queries.reshape(tok_rows, QUERY_HEADS, HEAD_DIM), cosine_table, -sine_values
    ).astype(bf16)
    d_key_b = apply_rotation(
        d_kv_own[:, :kv_width].reshape(tok_rows, KEY_HEADS, HEAD_DIM), cosine_table, -sine_values
    ).astype(bf16)
    d_proj = jnp.concatenate(
        [
            d_query_b.reshape(tok_rows, q_width),
            d_key_b.reshape(tok_rows, kv_width),
            d_kv_own[:, kv_width:].astype(bf16),
        ],
        axis=1,
    )
    qkv_all = jnp.concatenate(qkv_pieces, axis=0)
    d_normed_one = dot(d_proj, qkv_all[:, :gain_col], ((1,), (1,)))
    d_tok_rel, grad_gain_one = norm_backward(d_normed_one, unit_one, scale_one, gain_one)
    high = d_tok_rel.astype(bf16)
    low = (d_tok_rel - high.astype(f32)).astype(bf16)
    d_tokens = d_hidden + dot(high, shuffle, ((1,), (1,))) + dot(low, shuffle, ((1,), (1,)))
    grad_small = jnp.concatenate(
        [
            grad_router_rel,
            grad_gain_one[:, None],
            gain_two_rel[:, None],
            jnp.zeros((width, PAD - experts_total - 2), f32),
        ],
        axis=1,
    )
    summed_qkv = scatter_all(
        dot(first_normed[:, :half_width], d_proj, ((0,), (0,))),
        dot(first_normed[:, half_width:], d_proj, ((0,), (0,))).astype(bf16),
        own_rows,
        dp_count,
    )
    summed_small = scatter_all(grad_small[:half_width], grad_small[half_width:], own_rows, dp_count)

    mixture = scatter_all(mix_own, mix_other, tok_rows, planes, (grad_attended, d_proj))
    block_out = (hidden + mixture).astype(bf16)

    in_sent, out_sent = after((in_sent, out_sent), d_proj)
    in_back, out_back = [None] * planes, [None] * planes
    for k in range(dp_count):
        j = k % planes
        for back_list, sent in ((in_back, in_sent), (out_back, out_sent)):
            piece = sent[k].astype(f32)
            back_list[j] = piece if back_list[j] is None else back_list[j] + piece
    d_expert_in = jnp.concatenate(ordered(in_back, group_at), axis=0)
    d_expert_out = jnp.concatenate(ordered(out_back, group_at), axis=0)
    return (
        block_out,
        d_tokens,
        summed_small[:, experts_total],
        summed_qkv[:, :q_width],
        summed_qkv[:, q_width : q_width + kv_width],
        summed_qkv[:, q_width + kv_width : gain_col],
        summed_output,
        summed_small[:, experts_total + 1],
        summed_small[:, :experts_total],
        d_expert_in,
        d_expert_out,
    )


def solution(mesh):
    in_specs = (
        P(("dp", "fsdp"), None),
        P("dp", None),
        P(("dp", "fsdp"), None),
        P(("dp", "fsdp")),
        P(("dp", "fsdp"), None),
        P(("dp", "fsdp"), None),
        P(("dp", "fsdp"), None),
        P(("dp", "fsdp"), None),
        P(("dp", "fsdp")),
        P(("dp", "fsdp"), None),
        P("fsdp", "dp", None),
        P("fsdp", None, "dp"),
        P(("dp", "fsdp"), None),
    )
    out_specs = (
        P(("dp", "fsdp"), None),
        P(("dp", "fsdp"), None),
        P(("dp", "fsdp")),
        P(("dp", "fsdp"), None),
        P(("dp", "fsdp"), None),
        P(("dp", "fsdp"), None),
        P(("dp", "fsdp"), None),
        P(("dp", "fsdp")),
        P(("dp", "fsdp"), None),
        P("fsdp", "dp", None),
        P("fsdp", None, "dp"),
    )
    return jax.shard_map(local, mesh=mesh, in_specs=in_specs, out_specs=out_specs, check_vma=False)
```

```python
import math

import jax
import jax.numpy as jnp
from jax import lax
from jax.experimental import pallas as pl
from jax.experimental.pallas import tpu as pltpu
from jax.sharding import PartitionSpec as P


QUERY_HEADS = 16
KEY_HEADS = 8
HEAD_DIM = 64
CAP = 48
DP = "dp"
FSDP = "fsdp"
POOL_PLANES = 2
POOL_SHARDS = 16
PAD = 128


norm_eps = 1e-06
score_scale = 0.015625
rope_base = 10000.0
masked_low = -1e30

f32 = jnp.float32
bf16 = jnp.bfloat16


def swap(values, axis, mask):
    count = lax.axis_size(axis)
    return lax.ppermute(values, axis, [(i, i ^ mask) for i in range(count)])


def dot(left, right, dims):
    return lax.dot_general(left, right, (dims, ((), ())), preferred_element_type=f32)


def norm_backward(d_normed, unit_row, scale_row, gain_row):
    scaled = d_normed * gain_row
    grad_values = scale_row * (
        scaled - unit_row * jnp.mean(scaled * unit_row, axis=-1, keepdims=True)
    )
    return (grad_values, jnp.sum(d_normed * unit_row, axis=0))


def rope_tables(positions, head_size):
    half_index = jnp.arange(head_size // 2, dtype=f32)
    inverse = jnp.exp(half_index * (-2.0 * math.log(rope_base) / head_size))
    angles = positions.astype(f32)[:, None] * inverse[None, :]
    return (jnp.cos(angles), jnp.sin(angles))


def apply_rotation(values, cosine_table, sine_values):
    first_half, second_half = jnp.split(values, 2, axis=-1)
    cos_col = cosine_table[:, None, :]
    sin_col = sine_values[:, None, :]
    return jnp.concatenate(
        [
            first_half * cos_col - second_half * sin_col,
            second_half * cos_col + first_half * sin_col,
        ],
        axis=-1,
    )


def ordered(pieces, index):
    if len(pieces) == 1:
        return pieces
    half = len(pieces) // 2
    low, high = ordered(pieces[:half], index), ordered(pieces[half:], index)
    flip = (index & half) != 0
    return [jnp.where(flip, y, x) for x, y in zip(low, high)] + [
        jnp.where(flip, x, y) for x, y in zip(low, high)
    ]


def chip_masks():
    return [2 * c for c in range(1, lax.axis_size(FSDP) // 2)]


def gather_planes(rows, count):
    if count == 1:
        return rows
    step = lax.axis_size(DP) // count
    pieces = [rows] + [swap(rows, DP, k * step) for k in range(1, count)]
    return jnp.concatenate(pieces, axis=0)


def gather_pieces(rows, planes):
    first = gather_planes(rows, planes)
    half = [first] + [swap(first, FSDP, m) for m in chip_masks()]
    return half + [swap(piece, FSDP, 1) for piece in half]


def after(values, event):
    return values if event is None else lax.optimization_barrier((values, event))[0]


def scatter_chips(own_half, other_half, lead, event=None):
    total = own_half.astype(f32) + swap(other_half.astype(bf16), FSDP, 1).astype(
        f32
    )
    parts = total.astype(bf16)
    out = total[:lead]
    for c, m in enumerate(chip_masks(), 1):
        piece = swap(parts[c * lead : (c + 1) * lead], FSDP, m)
        piece = after(piece, event)
        out = out + piece.astype(f32)
    return out


def scatter_all(own_half, other_half, rows, count, events=(None, None)):
    step = lax.axis_size(DP) // count
    planes = scatter_chips(own_half, other_half, count * rows, events[0])
    parts = planes.astype(bf16)
    out = planes[:rows]
    for k in range(1, count):
        piece = swap(parts[k * rows : (k + 1) * rows], DP, k * step)
        out = out + after(piece, events[1]).astype(f32)
    return out


def gather_rows(rows, planes):
    first = gather_planes(rows, planes)
    half = jnp.concatenate([first] + [swap(first, FSDP, m) for m in chip_masks()], axis=0)
    return [half, swap(half, FSDP, 1)]


def expert_kernel(pieces, planes, held, tok_rows, width, ff, experts_total):
    blocks = pieces * planes
    half = pieces // 2
    contract_last = ((1,), (1,))
    contract_first = ((0,), (0,))

    def mm(left, right, dims=((1,), (0,))):
        return lax.dot_general(left, right, (dims, ((), ())), preferred_element_type=f32)

    def kernel(*refs):
        first_ref, router_ref, chosen_ref, slot_ref, win_ref, wout_ref = refs[:6]
        tok_refs = refs[6 : 6 + pieces]
        cot_refs = refs[6 + pieces : 6 + 2 * pieces]
        outs = refs[6 + 2 * pieces :]
        back_refs, mix_refs = outs[0:2], outs[2:4]
        gin_ref, gout_ref, rows_ref, drows_ref, gate_ref, back_rows_ref, mix_rows_ref = outs[4:]
        first = first_ref[0]
        slot_axis = lax.broadcasted_iota(jnp.int32, (CAP, tok_rows), 0)
        expert_axis = lax.broadcasted_iota(jnp.int32, (experts_total, planes * tok_rows), 0)

        def selection(block):
            return [slot_axis == slot_ref[block, e : e + 1, :] for e in range(held)]

        def stacked(parts):
            parts = [x.astype(f32) for x in parts]
            out = parts[0] if held == 1 else jnp.concatenate(parts, axis=0)
            return out.astype(bf16)

        for i in range(pieces):
            logits = mm(router_ref[...], tok_refs[i][...], contract_last)
            chosen = chosen_ref[i] > 0.0
            top = jnp.max(jnp.where(chosen, logits, masked_low), axis=0, keepdims=True)
            raised = jnp.where(chosen, jnp.exp(logits - top), 0.0)
            gates = raised / jnp.sum(raised, axis=0, keepdims=True)
            mine = [
                jnp.sum(jnp.where(expert_axis == first + e, gates, 0.0), axis=0, keepdims=True)
                for e in range(held)
            ]
            for a in range(planes):
                block = i * planes + a
                at = slice(a * tok_rows, (a + 1) * tok_rows)
                picks = selection(block)
                for e in range(held):
                    gate_ref[e, block * CAP : (block + 1) * CAP, :] = jnp.sum(
                        jnp.where(picks[e], mine[e][:, at], 0.0), axis=1, keepdims=True
                    )
                pick = stacked(picks)
                rows_ref[block] = mm(pick, tok_refs[i][at, :]).astype(bf16)
                drows_ref[block] = mm(pick, cot_refs[i][at, :width]).astype(bf16)

        lane = lax.broadcasted_iota(jnp.int32, (blocks * CAP, PAD), 1)
        for e in range(held):
            strip = slice(e * CAP, (e + 1) * CAP)
            rows = rows_ref[:, strip, :].reshape(blocks * CAP, width)
            gate = gate_ref[e]
            gate_up = mm(rows, win_ref[e])
            gate_part, up_part = gate_up[:, :ff], gate_up[:, ff:]
            sigmoid_g = 1.0 / (1.0 + jnp.exp(-gate_part))
            silu_g = gate_part * sigmoid_g
            activation = (silu_g * up_part).astype(bf16)
            result = mm(activation, wout_ref[e]).astype(bf16).astype(f32)
            mix_rows_ref[:, strip, :] = (gate * result).astype(bf16).reshape(blocks, CAP, width)
            d_rows = drows_ref[:, strip, :].reshape(blocks * CAP, width).astype(f32)
            d_gate = jnp.sum(d_rows * result, axis=1, keepdims=True)
            high = d_gate.astype(bf16).astype(f32)
            cols = jnp.where(
                lane == first + e,
                high,
                jnp.where(lane == first + e + experts_total, d_gate - high, 0.0),
            )
            back_rows_ref[:, strip, width:] = cols.astype(bf16).reshape(blocks, CAP, PAD)
            d_result = (gate * d_rows).astype(bf16)
            gout_ref[e] = mm(activation, d_result, contract_first).astype(bf16)
            d_act = mm(d_result, wout_ref[e], contract_last)
            d_gate_up = jnp.concatenate(
                [
                    d_act * up_part * sigmoid_g * (1.0 + gate_part * (1.0 - sigmoid_g)),
                    d_act * silu_g,
                ],
                axis=1,
            ).astype(bf16)
            back_rows_ref[:, strip, :width] = (
                mm(d_gate_up, win_ref[e], contract_last).astype(bf16).reshape(blocks, CAP, width)
            )
            gin_ref[e] = mm(rows, d_gate_up, contract_first).astype(bf16)

        for block in range(blocks):
            pick = stacked(selection(block))
            side, place = divmod(block, half * planes)
            at = slice(place * tok_rows, (place + 1) * tok_rows)
            back_refs[side][at, :] = mm(pick, back_rows_ref[block], contract_first).astype(bf16)
            mix_refs[side][at, :] = mm(pick, mix_rows_ref[block], contract_first).astype(bf16)

    side_rows = half * planes * tok_rows
    in_vmem = pl.BlockSpec(memory_space=pltpu.VMEM)
    return pl.pallas_call(
        kernel,
        out_shape=[jax.ShapeDtypeStruct((side_rows, width + PAD), bf16)] * 2
        + [jax.ShapeDtypeStruct((side_rows, width), bf16)] * 2
        + [
            jax.ShapeDtypeStruct((held, width, 2 * ff), bf16),
            jax.ShapeDtypeStruct((held, ff, width), bf16),
        ],
        in_specs=[pl.BlockSpec(memory_space=pltpu.SMEM)] + [in_vmem] * (5 + 2 * pieces),
        out_specs=[in_vmem] * 6,
        scratch_shapes=[
            pltpu.VMEM((blocks, held * CAP, width), bf16),
            pltpu.VMEM((blocks, held * CAP, width), bf16),
            pltpu.VMEM((held, blocks * CAP, 1), f32),
            pltpu.VMEM((blocks, held * CAP, width + PAD), bf16),
            pltpu.VMEM((blocks, held * CAP, width), bf16),
        ],
        compiler_params=pltpu.CompilerParams(vmem_limit_bytes=60 * 1024 * 1024),
        name="experts",
    )


def mm(left, right, dims=((1,), (0,))):
    return lax.dot_general(left, right, (dims, ((), ())), preferred_element_type=f32)


def project_kernel(pieces, piece_rows, rows, width, gain_col, rotated, q_width):
    def kernel(*refs):
        tokens_ref, scale_ref, shuffle_ref, cos_ref, sin_ref = refs[:5]
        piece_refs = refs[5 : 5 + pieces]
        unit_ref, normed_ref, gain_ref, q_ref, kv_ref = refs[5 + pieces :]
        unit = mm(tokens_ref[...], shuffle_ref[...]) * scale_ref[...]
        unit_ref[...] = unit
        projected = None
        for i, piece_ref in enumerate(piece_refs):
            at = slice(i * piece_rows, (i + 1) * piece_rows)
            gain = piece_ref[:, gain_col:].astype(f32).T[:1, :]
            gain_ref[:, at] = gain
            normed = (unit[:, at] * gain).astype(bf16)
            normed_ref[:, at] = normed
            part = mm(normed, piece_ref[:, :gain_col])
            projected = part if projected is None else projected + part
        lane = lax.broadcasted_iota(jnp.int32, (rows, PAD), 1)
        first_half = lane % HEAD_DIM < HEAD_DIM // 2
        cos, sin = cos_ref[...], sin_ref[...]
        for c in range(gain_col // PAD):
            at = slice(c * PAD, (c + 1) * PAD)
            x = projected[:, at]
            if c * PAD < rotated:
                other = jnp.where(
                    first_half,
                    -pltpu.roll(x, PAD - HEAD_DIM // 2, 1),
                    pltpu.roll(x, HEAD_DIM // 2, 1),
                )
                x = x * cos + other * sin
            if c * PAD < q_width:
                q_ref[:, at] = x.astype(bf16)
            else:
                kv_ref[:, c * PAD - q_width : (c + 1) * PAD - q_width] = x.astype(bf16)

    in_vmem = pl.BlockSpec(memory_space=pltpu.VMEM)
    return pl.pallas_call(
        kernel,
        out_shape=[
            jax.ShapeDtypeStruct((rows, width), f32),
            jax.ShapeDtypeStruct((rows, width), bf16),
            jax.ShapeDtypeStruct((1, width), f32),
            jax.ShapeDtypeStruct((rows, q_width), bf16),
            jax.ShapeDtypeStruct((rows, gain_col - q_width), bf16),
        ],
        in_specs=[in_vmem] * (5 + pieces),
        out_specs=[in_vmem] * 5,
        compiler_params=pltpu.CompilerParams(vmem_limit_bytes=40 * 1024 * 1024),
        name="proj",
    )


def rotate_back(x, cos, sin):
    lane = lax.broadcasted_iota(jnp.int32, x.shape, 1)
    other = jnp.where(
        lane % HEAD_DIM < HEAD_DIM // 2,
        pltpu.roll(x, PAD - HEAD_DIM // 2, 1),
        -pltpu.roll(x, HEAD_DIM // 2, 1),
    )
    return x * cos + other * sin


def back_project_kernel(pieces, piece_rows, rows, width, q_width, kv_width):
    gain_col = q_width + 2 * kv_width

    def kernel(dq_ref, dkv_ref, cos_ref, sin_ref, *refs):
        out_ref, dkv_out_ref = refs[pieces:]
        cos, sin = cos_ref[...], sin_ref[...]
        for c in range(kv_width // PAD):
            at = slice(c * PAD, (c + 1) * PAD)
            dkv_out_ref[:, at] = rotate_back(dkv_ref[:, at], cos, sin).astype(bf16)
        dkv_out_ref[:, kv_width:] = dkv_ref[:, kv_width:].astype(bf16)
        for i in range(pieces):
            out_ref[:, i * piece_rows : (i + 1) * piece_rows] = mm(
                dq_ref[...], refs[i][:, :q_width], ((1,), (1,))
            ) + mm(dkv_out_ref[...], refs[i][:, q_width:gain_col], ((1,), (1,)))

    in_vmem = pl.BlockSpec(memory_space=pltpu.VMEM)
    return pl.pallas_call(
        kernel,
        out_shape=[
            jax.ShapeDtypeStruct((rows, width), f32),
            jax.ShapeDtypeStruct((rows, 2 * kv_width), bf16),
        ],
        in_specs=[in_vmem] * (4 + pieces),
        out_specs=[in_vmem] * 2,
        compiler_params=pltpu.CompilerParams(vmem_limit_bytes=40 * 1024 * 1024),
        name="backproj",
    )


def attention_back_kernel(rows, keys, width, q_width, kv_width):
    pair = q_width // kv_width
    contract_last = ((1,), (1,))
    half = keys // 2

    def kernel(
        dh_ref, own_ref, other_ref, shuffle_ref, att_ref, q_ref, kv_ref, lse_ref,
        key_pos_ref, q_pos_ref, start_ref, cos_ref, sin_ref, dq_ref, dkv_own_ref, dkv_other_ref,
    ):
        dh = dh_ref[...]
        do_rel = jnp.concatenate(
            [mm(dh, ref[:, :width], contract_last) for ref in (own_ref, other_ref)], axis=1
        ).astype(bf16)
        d_att = mm(do_rel, shuffle_ref[...], contract_last).astype(bf16)
        prod = (d_att.astype(f32) * att_ref[...].astype(f32)).T
        allowed = (key_pos_ref[...] <= q_pos_ref[...]) & (key_pos_ref[...] >= start_ref[...])
        cos, sin = cos_ref[...], sin_ref[...]

        def stacked(x):
            return jnp.concatenate(
                [x[:, r * HEAD_DIM : (r + 1) * HEAD_DIM] for r in range(pair)], axis=0
            )

        def one_head(g):
            at = slice(g * pair * HEAD_DIM, (g + 1) * pair * HEAD_DIM)
            q = stacked(q_ref[:, at])
            d_out = stacked(d_att[:, at])
            key = kv_ref[:, g * HEAD_DIM : (g + 1) * HEAD_DIM]
            val = kv_ref[:, kv_width + g * HEAD_DIM : kv_width + (g + 1) * HEAD_DIM]
            delta = jnp.concatenate(
                [
                    jnp.sum(
                        prod[(g * pair + r) * HEAD_DIM : (g * pair + r + 1) * HEAD_DIM],
                        axis=0,
                        keepdims=True,
                    )
                    for r in range(pair)
                ],
                axis=1,
            )
            scores = mm(key, q, contract_last) * score_scale
            probs = jnp.where(allowed, jnp.exp(scores - lse_ref[g : g + 1, :]), 0.0)
            d_probs = mm(val, d_out, contract_last)
            d_scores = (probs * (d_probs - delta) * score_scale).astype(bf16)
            dq = mm(d_scores, key, ((0,), (0,)))
            dq = jnp.concatenate([dq[r * rows : (r + 1) * rows] for r in range(pair)], axis=1)
            for c in range(pair * HEAD_DIM // PAD):
                lanes = slice(c * PAD, (c + 1) * PAD)
                dq_ref[:, at.start + c * PAD : at.start + (c + 1) * PAD] = rotate_back(
                    dq[:, lanes], cos, sin
                ).astype(bf16)
            return mm(d_scores, q), mm(probs.astype(bf16), d_out)

        per_store = PAD // HEAD_DIM
        for c in range(kv_width // PAD):
            heads = [one_head(c * per_store + i) for i in range(per_store)]
            for j in range(2):
                both = jnp.concatenate([h[j] for h in heads], axis=1)
                lanes = slice(j * kv_width + c * PAD, j * kv_width + (c + 1) * PAD)
                dkv_own_ref[:, lanes] = both[:half]
                dkv_other_ref[:, lanes] = both[half:].astype(bf16)

    in_vmem = pl.BlockSpec(memory_space=pltpu.VMEM)
    return pl.pallas_call(
        kernel,
        out_shape=[
            jax.ShapeDtypeStruct((rows, q_width), bf16),
            jax.ShapeDtypeStruct((half, 2 * kv_width), f32),
            jax.ShapeDtypeStruct((half, 2 * kv_width), bf16),
        ],
        in_specs=[in_vmem] * 13,
        out_specs=[in_vmem] * 3,
        compiler_params=pltpu.CompilerParams(vmem_limit_bytes=56 * 1024 * 1024),
        name="attback",
    )


def attention_kernel(rows, keys, width, q_width, kv_width):
    pair = q_width // kv_width
    contract_last = ((1,), (1,))
    half = keys // 2

    def kernel(
        q_ref, first_ref, second_ref, key_pos_ref, q_pos_ref, start_ref, shuffle_ref, own_ref,
        other_ref, tokens_ref, gain_ref, att_ref, rel_ref, hidden_ref, unit_ref, normed_ref,
        scale_ref, lse_ref, kv_ref,
    ):
        kv_ref[:half] = first_ref[...]
        kv_ref[half:] = second_ref[...]
        allowed = (key_pos_ref[...] <= q_pos_ref[...]) & (key_pos_ref[...] >= start_ref[...])

        def one_head(g):
            at = g * pair * HEAD_DIM
            q = jnp.concatenate(
                [q_ref[:, at + r * HEAD_DIM : at + (r + 1) * HEAD_DIM] for r in range(pair)], axis=0
            )
            key = kv_ref[:, g * HEAD_DIM : (g + 1) * HEAD_DIM]
            val = kv_ref[:, kv_width + g * HEAD_DIM : kv_width + (g + 1) * HEAD_DIM]
            scores = jnp.where(allowed, mm(key, q, contract_last) * score_scale, masked_low)
            top = jnp.max(scores, axis=0, keepdims=True)
            raised = jnp.where(allowed, jnp.exp(scores - top), 0.0)
            total = jnp.sum(raised, axis=0, keepdims=True)
            lse_ref[g : g + 1, :] = top + jnp.log(total)
            probs = (raised / total).astype(bf16)
            out = mm(probs, val, ((0,), (0,)))
            att_ref[:, at : at + pair * HEAD_DIM] = jnp.concatenate(
                [out[r * rows : (r + 1) * rows] for r in range(pair)], axis=1
            ).astype(bf16)

        for g in range(kv_width // HEAD_DIM):
            one_head(g)
        rel = mm(att_ref[...], shuffle_ref[...]).astype(bf16)
        rel_ref[...] = rel
        hidden = tokens_ref[...].astype(f32) + (
            mm(rel[:, : width // 2], own_ref[:, :width])
            + mm(rel[:, width // 2 :], other_ref[:, :width])
        )
        hidden_ref[...] = hidden
        scale = lax.rsqrt(jnp.mean(hidden * hidden, axis=1, keepdims=True) + norm_eps)
        scale_ref[...] = scale
        unit = hidden * scale
        unit_ref[...] = unit
        normed_ref[...] = (unit * gain_ref[...]).astype(bf16)

    in_vmem = pl.BlockSpec(memory_space=pltpu.VMEM)
    return pl.pallas_call(
        kernel,
        out_shape=[
            jax.ShapeDtypeStruct((rows, q_width), bf16),
            jax.ShapeDtypeStruct((rows, q_width), bf16),
            jax.ShapeDtypeStruct((rows, width), f32),
            jax.ShapeDtypeStruct((rows, width), f32),
            jax.ShapeDtypeStruct((rows, width), bf16),
            jax.ShapeDtypeStruct((rows, 1), f32),
            jax.ShapeDtypeStruct((kv_width // HEAD_DIM, pair * rows), f32),
            jax.ShapeDtypeStruct((keys, 2 * kv_width), bf16),
        ],
        in_specs=[in_vmem] * 11,
        out_specs=[in_vmem] * 8,
        compiler_params=pltpu.CompilerParams(vmem_limit_bytes=56 * 1024 * 1024),
        name="wo",
    )


def local(
    tokens,
    seq_starts,
    expert_ids,
    attn_gain,
    w_query,
    key_weight,
    value_weight,
    w_output,
    ffn_gain,
    w_router,
    expert_in,
    expert_out,
    d_out,
):
    fsdp_count = lax.axis_size(FSDP)
    dp_count = lax.axis_size(DP)
    fsdp_at = lax.axis_index(FSDP)
    dp_at = lax.axis_index(DP)
    chips = fsdp_count // 2
    tok_rows, width = tokens.shape
    own_rows = w_query.shape[0]
    local_experts, slice_width, ff_two = expert_in.shape
    ff = ff_two // 2
    experts_total = w_router.shape[1]
    planes = POOL_PLANES
    if local_experts % planes or dp_count % planes or planes * fsdp_count > POOL_SHARDS:
        planes = 1
    held = local_experts // planes
    heads_per_key = QUERY_HEADS // KEY_HEADS
    q_width = QUERY_HEADS * HEAD_DIM
    kv_width = KEY_HEADS * HEAD_DIM

    pack_one = jnp.concatenate(
        [w_query, key_weight, value_weight, attn_gain[:, None], jnp.zeros((own_rows, PAD - 1), bf16)],
        axis=1,
    )
    pack_two = jnp.concatenate(
        [
            w_output,
            w_router,
            ffn_gain[:, None],
            jnp.zeros((own_rows, PAD - experts_total - 1), bf16),
        ],
        axis=1,
    )
    qkv_pieces = gather_pieces(pack_one, dp_count)
    output_own, output_other = gather_rows(pack_two, dp_count)

    rel = jnp.arange(width, dtype=jnp.int32)
    rel_row = rel % own_rows
    rel_dp = (rel // own_rows) % dp_count
    rel_chip = (rel // (own_rows * dp_count)) % chips
    rel_core = rel // (own_rows * dp_count * chips)
    place = (
        (rel_dp ^ dp_at) * fsdp_count + ((2 * rel_chip + rel_core) ^ fsdp_at)
    ) * own_rows + rel_row
    shuffle = (place[None, :] == jnp.arange(width, dtype=jnp.int32)[:, None]).astype(bf16)
    half_width = width // 2

    small_own, small_other = output_own[:, width:], output_other[:, width:]
    small_all = (
        dot(shuffle[:, :half_width], small_own, ((1,), (0,)))
        + dot(shuffle[:, half_width:], small_other, ((1,), (0,)))
    ).astype(bf16)
    router_w = small_all[:, :experts_total]
    gain_two = small_all[:, experts_total].astype(f32)[None, :]

    d_pack = jnp.concatenate(
        [d_out, expert_ids.astype(bf16), jnp.zeros((tok_rows, PAD - expert_ids.shape[1]), bf16)],
        axis=1,
    )
    d_pool = gather_pieces(d_pack, planes)

    top = dp_count // planes
    group_at = dp_at // top
    low_bits = [1 << i for i in range(top.bit_length() - 1)]
    in_groups = expert_in.reshape(planes, held, slice_width, ff_two)
    out_groups = expert_out.reshape(planes, held, ff, slice_width)
    in_parts, out_parts = {}, {}
    for groups, parts in ((in_groups, in_parts), (out_groups, out_parts)):
        parts[0] = lax.dynamic_index_in_dim(groups, group_at, 0, keepdims=False)
        for j in range(1, planes):
            away = lax.dynamic_index_in_dim(groups, group_at ^ j, 0, keepdims=False)
            parts[j * top] = swap(away, DP, j * top)
        for bit in low_bits:
            for k in sorted(parts):
                parts[k | bit] = swap(parts[k], DP, bit)
    out_parts = [out_parts[k] for k in range(dp_count)]

    token_index = jnp.arange(tok_rows, dtype=jnp.int32)
    global_pos = fsdp_at * tok_rows + token_index
    second_start = seq_starts[0, 1]
    sequence_start = jnp.where(global_pos >= second_start, second_start, seq_starts[0, 0])
    cosine_table, sine_values = rope_tables(global_pos - sequence_start, HEAD_DIM)
    tok_f32 = tokens.astype(f32)
    scale_one = lax.rsqrt(jnp.mean(tok_f32 * tok_f32, axis=-1, keepdims=True) + norm_eps)
    gain_col = q_width + 2 * kv_width
    piece_rows = qkv_pieces[0].shape[0]
    wide = (1, 2 * PAD // HEAD_DIM)
    cos_wide, sin_wide = jnp.tile(cosine_table, wide), jnp.tile(sine_values, wide)
    if piece_rows % PAD == 0:
        run = project_kernel(
            len(qkv_pieces), piece_rows, tok_rows, width, gain_col, q_width + kv_width, q_width
        )
        wide = (1, 2 * PAD // HEAD_DIM)
        unit_one, first_normed, gain_one, query_rows, kv_rows = run(
            tokens,
            scale_one,
            shuffle,
            cos_wide,
            sin_wide,
            *qkv_pieces,
        )
    else:
        unit_one = dot(tokens, shuffle, ((1,), (0,))) * scale_one
        gain_one = jnp.concatenate([piece[:, gain_col] for piece in qkv_pieces]).astype(f32)[None, :]
        first_normed = (unit_one * gain_one).astype(bf16)
        projected = sum(
            dot(first_normed[:, i * piece.shape[0] : (i + 1) * piece.shape[0]], piece, ((1,), (0,)))
            for i, piece in enumerate(qkv_pieces)
        )
        query_rows = apply_rotation(
            projected[:, :q_width].reshape(tok_rows, QUERY_HEADS, HEAD_DIM), cosine_table, sine_values
        ).astype(bf16)
        key_rows = apply_rotation(
            projected[:, q_width : q_width + kv_width].reshape(tok_rows, KEY_HEADS, HEAD_DIM),
            cosine_table,
            sine_values,
        ).astype(bf16)
        value_rows = projected[:, q_width + kv_width : q_width + 2 * kv_width].astype(bf16)
        kv_rows = jnp.concatenate([key_rows.reshape(tok_rows, kv_width), value_rows], axis=1)
    kv_first, kv_second = gather_rows(kv_rows, 1)
    shard = jnp.arange(fsdp_count, dtype=jnp.int32)
    shard_dev = (2 * (shard % chips) + shard // chips) ^ fsdp_at
    key_pos = (shard_dev[:, None] * tok_rows + token_index[None, :]).reshape(-1)
    pair = (1, heads_per_key)
    key_column = key_pos[:, None]
    q_row, start_row = jnp.tile(global_pos[None], pair), jnp.tile(sequence_start[None], pair)
    run = attention_kernel(tok_rows, key_pos.shape[0], width, q_width, kv_width)
    (
        attended_rows,
        attended_rel,
        hidden,
        unit_two,
        normed_two,
        scale_two,
        lse,
        kv_all,
    ) = run(
        query_rows.reshape(tok_rows, q_width),
        kv_first,
        kv_second,
        key_column,
        q_row,
        start_row,
        shuffle,
        output_own,
        output_other,
        tokens,
        gain_two,
    )

    normed_pool = gather_pieces(normed_two, planes)
    win = jnp.zeros((held, width, ff_two), bf16)
    for k in range(dp_count):
        win = lax.dynamic_update_slice(win, in_parts[k], (0, (dp_at ^ k) * slice_width, 0))
    wout = jnp.concatenate(ordered(out_parts, dp_at), axis=2)
    expert_axis = jnp.arange(experts_total, dtype=jnp.int32)
    first_expert = fsdp_at * local_experts + group_at * held
    my_experts = first_expert + jnp.arange(held, dtype=jnp.int32)
    lower = (token_index[:, None] > token_index[None, :]).astype(bf16)

    def dense_gates(rows, chosen):
        logits = dot(rows, router_w, ((1,), (0,)))
        top = jnp.max(jnp.where(chosen, logits, masked_low), axis=-1, keepdims=True)
        raised = jnp.where(chosen, jnp.exp(logits - top), 0.0)
        return raised / jnp.sum(raised, axis=-1, keepdims=True)

    def chosen_of(ids):
        return jnp.any(ids[:, :, None] == expert_axis[None, None, :], axis=1)

    pieces = len(normed_pool)
    ids_all = jnp.stack([x[:, width : width + expert_ids.shape[1]] for x in d_pool])
    ids_all = ids_all.astype(jnp.int32)
    chosen_rows = (
        jnp.any(ids_all[:, None] == expert_axis[None, :, None, None], axis=-1).astype(f32)
    )
    mine = jnp.any(ids_all[:, None] == my_experts[None, :, None, None], axis=-1)
    mine = mine.reshape(pieces, held, planes, tok_rows)
    before = jnp.einsum(
        "iepu,tu->iept", mine.astype(bf16), lower, preferred_element_type=f32
    ).astype(jnp.int32)
    slots = jnp.where(mine, before, -1).transpose(0, 2, 1, 3).reshape(-1, held, tok_rows)
    run = expert_kernel(pieces, planes, held, tok_rows, width, ff, experts_total)
    back_own, back_other, mix_own, mix_other, grad_in_b, grad_out_b = run(
        first_expert[None], router_w.T, chosen_rows, slots, win, wout, *normed_pool, *d_pool
    )
    back = scatter_all(back_own, back_other, tok_rows, planes)

    in_sent, out_sent, in_near, out_near = [], [], [], []
    for grads, axis, sent, near in (
        (grad_in_b, 1, in_sent, in_near), (grad_out_b, 2, out_sent, out_near)
    ):
        left = {
            k: lax.dynamic_slice_in_dim(grads, (dp_at ^ k) * slice_width, slice_width, axis)
            for k in range(dp_count)
        }
        for bit in reversed(low_bits):
            for k in sorted(left, reverse=True):
                if k & bit:
                    moved = swap(left.pop(k), DP, bit)
                    if k == bit:
                        near.append(moved)
                        continue
                    kept = left[k ^ bit].astype(f32) + moved.astype(f32)
                    left[k ^ bit] = kept.astype(bf16) if k >= top else kept
        sent.append(left[0])
        for j in range(1, planes):
            sent.append(swap(left[j * top].astype(bf16), DP, j * top))

    d_block = d_out.astype(f32)
    d_gate = (
        back[:, width : width + experts_total]
        + back[:, width + experts_total : width + 2 * experts_total]
    )
    gates = dense_gates(normed_two, chosen_of(expert_ids))
    d_logits = (gates * (d_gate - jnp.sum(gates * d_gate, axis=-1, keepdims=True))).astype(bf16)
    d_normed_two = back[:, :width] + dot(d_logits, router_w, ((1,), (1,)))
    d_hidden_two, grad_gain_two = norm_backward(d_normed_two, unit_two, scale_two, gain_two)
    d_hidden = d_block + d_hidden_two
    d_hidden_b = d_hidden.astype(bf16)
    normed_two_rel = dot(normed_two, shuffle, ((1,), (0,))).astype(bf16)
    gain_two_high = grad_gain_two.astype(bf16)
    gain_two_low = (grad_gain_two - gain_two_high.astype(f32)).astype(bf16)
    gain_two_rel = jnp.sum(
        dot(jnp.stack([gain_two_high, gain_two_low]), shuffle, ((1,), (0,))), axis=0
    )
    grad_output_own = dot(attended_rel[:, :half_width], d_hidden_b, ((0,), (0,)))
    grad_output_other = dot(attended_rel[:, half_width:], d_hidden_b, ((0,), (0,))).astype(bf16)
    grad_router_rel = dot(normed_two_rel, d_logits, ((0,), (0,)))

    run = attention_back_kernel(tok_rows, key_pos.shape[0], width, q_width, kv_width)
    d_query_b, d_kv_first, d_kv_second = run(
        d_hidden_b,
        output_own,
        output_other,
        shuffle,
        attended_rows,
        query_rows.reshape(tok_rows, q_width),
        kv_all,
        lse,
        key_column,
        q_row,
        start_row,
        cos_wide,
        sin_wide,
    )
    d_kv_own = scatter_chips(d_kv_first, d_kv_second, tok_rows)
    summed_output = scatter_all(grad_output_own, grad_output_other, own_rows, dp_count)
    if piece_rows % PAD == 0:
        run = back_project_kernel(
            len(qkv_pieces), piece_rows, tok_rows, width, q_width, kv_width
        )
        d_normed_one, d_kv_b = run(d_query_b, d_kv_own, cos_wide, sin_wide, *qkv_pieces)
    else:
        d_key_b = apply_rotation(
            d_kv_own[:, :kv_width].reshape(tok_rows, KEY_HEADS, HEAD_DIM), cosine_table, -sine_values
        ).reshape(tok_rows, kv_width)
        d_kv_b = jnp.concatenate([d_key_b, d_kv_own[:, kv_width:]], axis=1).astype(bf16)
        d_proj = jnp.concatenate([d_query_b, d_kv_b], axis=1)
        qkv_all = jnp.concatenate(qkv_pieces, axis=0)
        d_normed_one = dot(d_proj, qkv_all[:, :gain_col], ((1,), (1,)))
    d_tok_rel, grad_gain_one = norm_backward(d_normed_one, unit_one, scale_one, gain_one)
    high = d_tok_rel.astype(bf16)
    low = (d_tok_rel - high.astype(f32)).astype(bf16)
    d_tokens = d_hidden + dot(high, shuffle, ((1,), (1,))) + dot(low, shuffle, ((1,), (1,)))
    grad_small = jnp.concatenate(
        [
            grad_router_rel,
            grad_gain_one[:, None],
            gain_two_rel[:, None],
            jnp.zeros((width, PAD - experts_total - 2), f32),
        ],
        axis=1,
    )
    normed_own, normed_other = first_normed[:, :half_width], first_normed[:, half_width:]
    summed_q, summed_kv = [
        scatter_all(
            dot(normed_own, d_rows, ((0,), (0,))),
            dot(normed_other, d_rows, ((0,), (0,))).astype(bf16),
            own_rows,
            dp_count,
        )
        for d_rows in (d_query_b, d_kv_b)
    ]
    summed_small = scatter_all(grad_small[:half_width], grad_small[half_width:], own_rows, dp_count)

    mixture = scatter_all(mix_own, mix_other, tok_rows, planes, (d_query_b, d_kv_b))
    block_out = (hidden + mixture).astype(bf16)

    in_sent, out_sent, in_near, out_near = after((in_sent, out_sent, in_near, out_near), d_kv_b)
    in_back = [piece.astype(f32) for piece in in_sent]
    out_back = [piece.astype(f32) for piece in out_sent]
    in_back[0] = sum((piece.astype(f32) for piece in in_near), in_back[0])
    out_back[0] = sum((piece.astype(f32) for piece in out_near), out_back[0])
    group_axis = jnp.arange(planes, dtype=jnp.int32)[:, None, None, None] ^ group_at
    totals = []
    for back_list in (in_back, out_back):
        total = back_list[0][None]
        for j in range(1, planes):
            total = jnp.where(group_axis == j, back_list[j][None], total)
        total = jnp.broadcast_to(total, (planes,) + back_list[0].shape)
        totals.append(total.reshape((local_experts,) + back_list[0].shape[1:]))
    d_expert_in, d_expert_out = totals
    return (
        block_out,
        d_tokens,
        summed_small[:, experts_total],
        summed_q,
        summed_kv[:, :kv_width],
        summed_kv[:, kv_width:],
        summed_output,
        summed_small[:, experts_total + 1],
        summed_small[:, :experts_total],
        d_expert_in,
        d_expert_out,
    )


def solution(mesh):
    in_specs = (
        P((DP, FSDP), None),
        P(DP, None),
        P((DP, FSDP), None),
        P((DP, FSDP)),
        P((DP, FSDP), None),
        P((DP, FSDP), None),
        P((DP, FSDP), None),
        P((DP, FSDP), None),
        P((DP, FSDP)),
        P((DP, FSDP), None),
        P(FSDP, DP, None),
        P(FSDP, None, DP),
        P((DP, FSDP), None),
    )
    out_specs = (
        P((DP, FSDP), None),
        P((DP, FSDP), None),
        P((DP, FSDP)),
        P((DP, FSDP), None),
        P((DP, FSDP), None),
        P((DP, FSDP), None),
        P((DP, FSDP), None),
        P((DP, FSDP)),
        P((DP, FSDP), None),
        P(FSDP, DP, None),
        P(FSDP, None, DP),
    )
    return jax.shard_map(local, mesh=mesh, in_specs=in_specs, out_specs=out_specs, check_vma=False)
```
